32 devices in a mesh: grp: 2 (over y), ctx: 4 (over z), head: 4 (over x, core).
Axes of the slice: x: 2, y: 2, z: 4, core: 2. Of those that a mesh axis runs over, the one named last changes fastest.
Arguments:
- behavior_embed: bfloat16 [4, 2048, 256], P('grp', 'ctx'), parts along dimension 0, may hold values from -6 to 6
- behavior_mask: int32 [4, 2048], P('grp', 'ctx'), parts along dimension 0, may hold values 0 or 1
- history_len: int32 [4], P('grp'), parts along dimension 0, may hold values from 256 to 2048, as said below
- log_decay: float32 [8, 4, 2048], P('head', 'grp', 'ctx'), parts along dimension 1, may hold values from -2 to 0
- candidate_embed: bfloat16 [4, 512, 256], P('grp', 'ctx'), parts along dimension 0, may hold values from -6 to 6
- input_weight: bfloat16 [256, 1024], replicated, may hold values from -0.375 to 0.375
- input_gain: float32 [1024], replicated, may hold values from 0.5 to 1.5
- proj_weight: bfloat16 [4, 1024, 1024], P(None, None, 'head'), may hold values from -0.1875 to 0.1875
- output_gain: float32 [1024], P('head'), may hold values from 0.5 to 1.5
- ranker_first: bfloat16 [1024, 1024], P('head'), may hold values from -0.1875 to 0.1875
- ranker_second: bfloat16 [1024], replicated, may hold values from -0.1875 to 0.1875
Outputs:
- history_out: bfloat16 [4, 2048, 1024], P('grp', 'ctx', 'head'), parts along dimension 0
- scores: float32 [4, 512], P('grp', ('ctx', 'head')), parts along dimension 0
The draws below stay inside these ranges and needn't reach their ends.
There are 2 independent parts, one for each index of `grp`. The reference program is written for one: setup_inputs(seed, part) draws one part's arguments, and reference() takes and returns one part's arrays. A program takes and returns all parts, laid end to end along the dimension named above; an argument that names none is the same for every part. Nothing has to cross between parts.
Inputs may be any that keep to these rules, and one draw needn't show every extreme that they name: Histories are padded at the start: the last history_len[u] positions hold user u's behaviors; at least one user's history fills all 2048 positions.
All inputs are finite; a program needn't handle non-finite values. No bound on the sum of `behavior_mask` on one device may be relied on, other than what follows from the above.
Results may differ from the reference program's by a relative error of at most 0.0098.
Values may be sent and summed in bfloat16 or wider, within the bound.
No kernel may reach another device: no remote copies, remote signals or barrier semaphores. Data moves between devices by JAX's collectives and lax.ppermute only.
A program may use at most 64 MiB of HBM per device.

```python
import math
import jax
import jax.numpy as jnp
from jax import lax

USER_GROUP_SIZE = 2
L_DEV = 512
HEAD_TOTAL = 8
DH = 128
D = 1024
E = 256
MLP_H = 1024
BEHAVIOR_LENGTH = 2048
CAND = 512


def draw_log_decay(key, part):
    random_subkeys = jax.random.split(key, 7)
    fast_share = 0.5
    slow_low = math.log(0.1)
    slow_high = math.log(0.4)
    fast_head = jax.random.uniform(random_subkeys[0], (HEAD_TOTAL, 1, 1)) < fast_share
    fast_rate = jnp.exp(jax.random.uniform(random_subkeys[1], (HEAD_TOTAL, 1, 1), minval=-0.3, maxval=0.3)) / 40.0
    slow_rate = jnp.exp(jax.random.uniform(random_subkeys[2], (HEAD_TOTAL, 1, 1), minval=slow_low, maxval=slow_high)) * math.log(10.0) / BEHAVIOR_LENGTH
    per_position_rate = jnp.where(fast_head, fast_rate, slow_rate)
    segment_count = BEHAVIOR_LENGTH // L_DEV
    segment_weight = jnp.exp(jax.random.uniform(random_subkeys[3], (1, USER_GROUP_SIZE, segment_count, 1), minval=-0.7, maxval=0.7))
    segment_weight = jnp.broadcast_to(segment_weight, (1, USER_GROUP_SIZE, segment_count, L_DEV)).reshape(1, USER_GROUP_SIZE, BEHAVIOR_LENGTH)
    position_weight = jnp.exp(jax.random.uniform(random_subkeys[4], (HEAD_TOTAL, USER_GROUP_SIZE, BEHAVIOR_LENGTH), minval=-0.7, maxval=0.7))
    spike_location = jax.random.randint(random_subkeys[5], (HEAD_TOTAL, USER_GROUP_SIZE, 2), 0, BEHAVIOR_LENGTH)
    spike_length = jnp.log(jax.random.uniform(random_subkeys[6], (HEAD_TOTAL, USER_GROUP_SIZE, 2), minval=0.5, maxval=0.8))
    position_indices = jnp.arange(BEHAVIOR_LENGTH, dtype=jnp.int32)
    activity_spikes = jnp.sum(jnp.where(position_indices[None, None, None, :] == spike_location[..., None], spike_length[..., None], 0.0), axis=2)
    return (-per_position_rate * segment_weight * position_weight + activity_spikes).astype(jnp.float32)


def draw_history_len(key, part):
    random_subkeys = jax.random.split(key, 2)
    lengths = jax.random.randint(random_subkeys[0], (USER_GROUP_SIZE,), BEHAVIOR_LENGTH // 8, BEHAVIOR_LENGTH + 1)
    full_user = jax.random.randint(random_subkeys[1], (), 0, USER_GROUP_SIZE)
    return jnp.where(jnp.arange(USER_GROUP_SIZE) == full_user, BEHAVIOR_LENGTH, lengths).astype(jnp.int32)


def set_ends(array, stream_key, least, high):
    spot = [jax.random.randint(jax.random.fold_in(stream_key, axis), (), 0, length) for axis, length in enumerate(array.shape)]
    widest = array.shape.index(max(array.shape))
    beside = spot[:widest] + [(spot[widest] + 1) % array.shape[widest]] + spot[widest + 1:]
    return array.at[tuple(spot)].set(least).at[tuple(beside)].set(high)


def block_levels(stream_key, extent, cuts, low, largest):
    def one(position, blocks):
        draws = jax.random.uniform(jax.random.fold_in(jax.random.fold_in(stream_key, 6), position), (blocks,), jnp.float32, low / len(cuts), largest / len(cuts))
        return jnp.repeat(jnp.exp(draws), extent[position] // blocks).reshape((-1,) + (1,) * (len(extent) - position - 1))

    factor_of = one(*cuts[0])
    for cut in cuts[1:]:
        factor_of = factor_of * one(*cut)
    return factor_of


def bell_draw(stream_key, dims, deviation, most, shards=(), kind=jnp.bfloat16):
    level = block_levels(stream_key, dims, shards, -0.22, 0.18) if shards else 1.0
    values = jax.random.normal(stream_key, dims, jnp.float32) * deviation * level
    return jnp.minimum(jnp.maximum(values, -most), most).astype(kind)


def setup_inputs(seed: int = 0, part: int = 0) -> dict:
    arg_keys = jax.random.split(jax.random.key(seed), 12)
    part_splits = jax.random.split(jax.random.fold_in(arg_keys[11], part), 12)
    return {
        "behavior_embed": bell_draw(part_splits[0], (USER_GROUP_SIZE, BEHAVIOR_LENGTH, E), 1.0, 6.0, ((1, 4),)),
        "behavior_mask": set_ends((jax.random.randint(part_splits[1], (USER_GROUP_SIZE, BEHAVIOR_LENGTH), 0, 8) < 7).astype(jnp.int32), jax.random.fold_in(part_splits[1], 1), 0, 1),
        "history_len": draw_history_len(jax.random.fold_in(jax.random.fold_in(arg_keys[11], part), 71), part),
        "log_decay": draw_log_decay(jax.random.fold_in(jax.random.fold_in(arg_keys[11], part), 71), part),
        "candidate_embed": bell_draw(part_splits[4], (USER_GROUP_SIZE, CAND, E), 1.0, 6.0, ((1, 4),)),
        "input_weight": bell_draw(arg_keys[5], (E, D), E ** -0.5, 0.375),
        "input_gain": jnp.clip(1.0 + 0.1 * jax.random.normal(arg_keys[6], (D,), jnp.float32), 0.5, 1.5),
        "proj_weight": bell_draw(arg_keys[7], (4, D, D), D ** -0.5, 0.1875, ((2, 4),)),
        "output_gain": jnp.clip(1.0 + 0.1 * jax.random.normal(arg_keys[8], (D,), jnp.float32), 0.5, 1.5),
        "ranker_first": bell_draw(arg_keys[9], (D, MLP_H), D ** -0.5, 0.1875, ((0, 4),)),
        "ranker_second": bell_draw(arg_keys[10], (MLP_H,), MLP_H ** -0.5, 0.1875),
    }


epsilon = 1e-05
highest = lax.Precision.HIGHEST

def rms_norm(values, gain_row):
    mean_square = lax.optimization_barrier(jnp.mean(values * values, axis=-1, keepdims=True))
    return values * lax.rsqrt(mean_square + epsilon) * gain_row

def features(embed_rows, input_weight, input_gain):
    embedded = embed_rows.reshape(-1, embed_rows.shape[-1])
    rounded = lax.optimization_barrier(jnp.dot(embedded, input_weight, preferred_element_type=jnp.float32).astype(jnp.bfloat16))
    return rms_norm(rounded.astype(jnp.float32), input_gain).astype(jnp.bfloat16)

def reference(behavior_embed, behavior_mask, history_len, log_decay, candidate_embed, input_weight, input_gain, proj_weight, output_gain, ranker_first, ranker_second):
    position_indices = jnp.arange(BEHAVIOR_LENGTH, dtype=jnp.int32)
    valid_mask = ((position_indices[None, :] >= BEHAVIOR_LENGTH - history_len[:, None]) & (behavior_mask == 1)).astype(jnp.float32)
    behavior_norm = features(behavior_embed, input_weight, input_gain)
    candidate_norm = features(candidate_embed, input_weight, input_gain)
    query_rows = jnp.dot(behavior_norm, proj_weight[0], preferred_element_type=jnp.float32).astype(jnp.bfloat16)
    key_rows = (jnp.dot(behavior_norm, proj_weight[1], preferred_element_type=jnp.float32) * DH ** (-0.5)).astype(jnp.bfloat16)
    value_rows = jnp.dot(behavior_norm, proj_weight[2], preferred_element_type=jnp.float32).astype(jnp.bfloat16)
    gate_rows = jnp.dot(behavior_norm, proj_weight[3], preferred_element_type=jnp.float32).astype(jnp.bfloat16)
    blocks = BEHAVIOR_LENGTH // L_DEV

    def by_block(rows):
        return jnp.transpose(rows.reshape(USER_GROUP_SIZE, blocks, L_DEV, HEAD_TOTAL, DH), (1, 0, 2, 3, 4)).astype(jnp.float32)
    decay_blocks = jnp.transpose(log_decay.reshape(HEAD_TOTAL, USER_GROUP_SIZE, blocks, L_DEV), (2, 0, 1, 3))
    mask_blocks = jnp.transpose(valid_mask.reshape(USER_GROUP_SIZE, blocks, L_DEV), (1, 0, 2))
    row_ids = jnp.arange(L_DEV)
    causal = row_ids[:, None] >= row_ids[None, :]

    def step_block(carry_state, inputs):
        query_block, key_block, value_block, decay_block, mask_block = inputs
        cumulative = jnp.cumsum(decay_block, axis=-1)
        span_total = cumulative[..., -1]
        log_gap = cumulative[..., :, None] - cumulative[..., None, :]
        decay_matrix = jnp.where(causal, jnp.exp(jnp.where(causal, log_gap, 0.0)), 0.0) * mask_block[None, :, None, :]
        scores_local = jnp.einsum('uihd,ujhd->huij', query_block, key_block, precision=highest)
        within = jnp.einsum('huij,ujhd->uihd', scores_local * decay_matrix, value_block, precision=highest)
        carried = jnp.einsum('uihd,hude->uihe', query_block, carry_state, precision=highest) * jnp.exp(jnp.transpose(cumulative, (1, 2, 0)))[..., None]
        key_weight = jnp.exp(span_total[..., None] - cumulative) * mask_block[None]
        local_state = jnp.einsum('ujhd,ujhe->hude', key_block * jnp.transpose(key_weight, (1, 2, 0))[..., None], value_block, precision=highest)
        next_state = jnp.exp(span_total)[..., None, None] * carry_state + local_state
        return (next_state, within + carried)
    initial = jnp.zeros((HEAD_TOTAL, USER_GROUP_SIZE, DH, DH), jnp.float32)
    final_full, readout = lax.scan(step_block, initial, (by_block(query_rows), by_block(key_rows), by_block(value_rows), decay_blocks, mask_blocks))
    readout = jnp.transpose(readout, (1, 0, 2, 3, 4)).reshape(USER_GROUP_SIZE, BEHAVIOR_LENGTH, HEAD_TOTAL, DH)
    gain_heads = output_gain.reshape(HEAD_TOTAL, DH)
    gate_wide = gate_rows.astype(jnp.float32).reshape(USER_GROUP_SIZE, BEHAVIOR_LENGTH, HEAD_TOTAL, DH)
    history_out = (rms_norm(readout, gain_heads) * jax.nn.silu(gate_wide)).reshape(USER_GROUP_SIZE, BEHAVIOR_LENGTH, D).astype(jnp.bfloat16)
    final_state = final_full.astype(jnp.bfloat16)
    candidate_query = jnp.dot(candidate_norm, proj_weight[0], preferred_element_type=jnp.float32).astype(jnp.bfloat16).reshape(USER_GROUP_SIZE, CAND, HEAD_TOTAL, DH)
    candidate_read = jnp.einsum('uchd,hude->uche', candidate_query.astype(jnp.float32), final_state.astype(jnp.float32), precision=highest)
    candidate_feat = (rms_norm(candidate_read, gain_heads).reshape(USER_GROUP_SIZE * CAND, D) + candidate_norm.astype(jnp.float32)).astype(jnp.bfloat16)
    hidden = jnp.dot(candidate_feat, ranker_first, preferred_element_type=jnp.float32)
    scores = jnp.dot(jax.nn.silu(hidden), ranker_second.astype(jnp.float32), precision=highest).reshape(USER_GROUP_SIZE, CAND)
    return (history_out, scores)
```

```python
import functools

import jax
import jax.numpy as jnp
from jax import lax
from jax.experimental import pallas as pl
from jax.experimental.pallas import tpu as pltpu
from jax.sharding import PartitionSpec as P

DH = 128
EPS = 1e-05
F32 = jnp.float32
BF16 = jnp.bfloat16
ANY = pl.BlockSpec(memory_space=pl.ANY)
HBM = pl.BlockSpec(memory_space=pltpu.HBM)
VMEM = pl.BlockSpec(memory_space=pltpu.VMEM)
SMEM = pl.BlockSpec(memory_space=pltpu.SMEM)


def dot(a, b):
    return jnp.dot(a, b, preferred_element_type=F32)


def dot_nt(a, b):
    return lax.dot_general(a, b, (((1,), (1,)), ((), ())), preferred_element_type=F32)


def dot_tn(a, b):
    return lax.dot_general(a, b, (((0,), (0,)), ((), ())), preferred_element_type=F32)


def scale_rms(values, gain):
    mean_square = jnp.mean(values * values, axis=-1, keepdims=True)
    return values * lax.rsqrt(mean_square + EPS) * gain


def call(kernel, outs, ins, in_specs, out_specs, scratch, name, flops, limit=24):
    total = sum(x.size * x.dtype.itemsize for x in ins)
    return pl.pallas_call(
        kernel,
        out_shape=outs,
        in_specs=in_specs,
        out_specs=out_specs,
        scratch_shapes=scratch,
        name=name,
        compiler_params=pltpu.CompilerParams(vmem_limit_bytes=limit << 20),
        cost_estimate=pl.CostEstimate(flops=flops, bytes_accessed=total, transcendentals=0),
    )(*ins)


def kernel_a(
    users, heads, span, seq_total,
    hist, mask, decay, emb_hbm, win_hbm, gain_ref, proj_hbm,
    norm_out, key_out, value_out, payload, cum_out, valid_out, cum_col_out,
    emb, win, wkv, rows8, sems,
):
    cols = heads * DH
    pairs = heads * users
    block = min(256, span)
    copies = []

    def fetch(src, dst, slot):
        copy = pltpu.make_async_copy(src, dst, sems.at[slot])
        copy.start()
        return copy

    get_win = fetch(win_hbm, win, 0)
    get_emb = [fetch(emb_hbm.at[u], emb.at[u], 1 + u) for u in range(users)]
    get_k = fetch(proj_hbm.at[1], wkv.at[0], 1 + users)
    get_v = fetch(proj_hbm.at[2], wkv.at[1], 2 + users)

    rows8[...] = jnp.zeros_like(rows8)
    for h in range(heads):
        rows8[h * users:(h + 1) * users, :] = decay[h]
    cum = rows8[...]
    lane = lax.broadcasted_iota(jnp.int32, cum.shape, 1)
    step = 1
    while step < span:
        cum = cum + jnp.where(lane >= step, pltpu.roll(cum, step, 1), 0.0)
        step *= 2
    cum_out[...] = cum
    position = lax.axis_index("ctx") * span + lax.broadcasted_iota(jnp.int32, (1, span), 1)
    for u in range(users):
        keep = (position >= seq_total - hist[u]) & (mask[u:u + 1, :] == 1)
        valid_out[u:u + 1, :] = jnp.where(keep, 1.0, 0.0)
    total = cum[:, span - 1:span]
    weight = jnp.exp(total - cum)
    weights = []
    for h in range(heads):
        for u in range(users):
            r = h * users + u
            weights.append(weight[r:r + 1, :] * valid_out[u:u + 1, :])
    for r in range(pairs):
        rows8[r:r + 1, :] = weights[r]
    weight_col = jnp.transpose(rows8[...])
    cum_col_out[...] = jnp.transpose(cum)

    state_rows = pairs * DH
    tail = payload.shape[0] - state_rows
    row_id = lax.broadcasted_iota(jnp.int32, (tail, DH), 0)
    logs = jnp.zeros((tail, DH), F32)
    for r in range(pairs):
        rest = jnp.broadcast_to(total[r:r + 1, :], (tail, DH))
        for t in range(3):
            part = rest.astype(BF16).astype(F32)
            logs = jnp.where(row_id == 3 * r + t, part, logs)
            rest = rest - part
    payload[state_rows:, :] = logs.astype(BF16)

    get_win.wait()
    for u in range(users):
        get_emb[u].wait()
        for b in range(span // block):
            rows = slice(u * span + b * block, u * span + (b + 1) * block)
            raw = dot(emb[u, b * block:(b + 1) * block, :], win[...]).astype(BF16).astype(F32)
            norm_out[rows, :] = scale_rms(raw, gain_ref[...][None, :]).astype(BF16)
        if u == 0:
            get_k.wait()
            get_v.wait()
        for b in range(span // block):
            rows = slice(u * span + b * block, u * span + (b + 1) * block)
            norm = norm_out[rows, :]
            key_out[rows, :] = (dot(norm, wkv[0]) * DH ** -0.5).astype(BF16)
            value_out[rows, :] = dot(norm, wkv[1]).astype(BF16)
        for h in range(heads):
            r = h * users + u
            rows = slice(u * span, (u + 1) * span)
            lanes = slice(h * DH, (h + 1) * DH)
            key = key_out[rows, lanes].astype(F32) * weight_col[:, r:r + 1]
            state = dot_tn(key.astype(BF16), value_out[rows, lanes])
            payload[r * DH:(r + 1) * DH, :] = state.astype(BF16)


def kernel_b(
    users, heads, span,
    norm_ref, key_ref, value_ref, cum, valid, cum_col, proj_hbm,
    cemb, win, gain_ref,
    query_out, gate_out, within_out, cquery_out, own_out,
    wq, wg, cnorm, sems,
):
    cols = heads * DH
    block = min(256, span)
    get_q = pltpu.make_async_copy(proj_hbm.at[0], wq, sems.at[0])
    get_g = pltpu.make_async_copy(proj_hbm.at[3], wg, sems.at[1])
    get_q.start()
    get_g.start()
    cands = cemb.shape[1]
    for u in range(users):
        raw = dot(cemb[u], win[...]).astype(BF16).astype(F32)
        cnorm[u * cands:(u + 1) * cands, :] = scale_rms(raw, gain_ref[...][None, :]).astype(BF16)
    start = pl.multiple_of(lax.axis_index("head") * cols, cols)
    own_out[...] = cnorm[:, pl.ds(start, cols)]
    get_q.wait()
    cquery_out[...] = dot(cnorm[...], wq[...]).astype(BF16)
    get_g.wait()
    for u in range(users):
        for b in range(span // block):
            rows = slice(u * span + b * block, u * span + (b + 1) * block)
            norm = norm_ref[rows, :]
            query_out[rows, :] = dot(norm, wq[...]).astype(BF16)
            gate_out[rows, :] = dot(norm, wg[...]).astype(BF16)
            width = (b + 1) * block
            seen = slice(u * span, u * span + width)
            row_id = b * block + lax.broadcasted_iota(jnp.int32, (block, width), 0)
            col_id = lax.broadcasted_iota(jnp.int32, (block, width), 1)
            keep = (row_id >= col_id) & (valid[u:u + 1, :width] > 0.0)
            for h in range(heads):
                r = h * users + u
                lanes = slice(h * DH, (h + 1) * DH)
                gap = cum_col[b * block:(b + 1) * block, r:r + 1] - cum[r:r + 1, :width]
                pair = dot_nt(query_out[rows, lanes], key_ref[seen, lanes])
                pair = pair * jnp.where(keep, jnp.exp(jnp.minimum(gap, 0.0)), 0.0)
                within_out[rows, lanes] = dot(pair.astype(BF16), value_ref[seen, lanes])


def kernel_c(users, heads, ctx_count, head_count, source, dest, *refs):
    received = refs[:ctx_count]
    cquery, own, gain_ref = refs[ctx_count:ctx_count + 3]
    outs = refs[ctx_count + 3:]
    prefix_out = outs[0]
    feat_outs = outs[1:1 + head_count]
    pieces, feat, sems = outs[1 + head_count:]
    me = lax.axis_index("ctx")
    copies = []
    for k in range(ctx_count):
        copy = pltpu.make_async_copy(received[k], pieces.at[source(me, k, ctx_count)], sems.at[k])
        copy.start()
        copies.append(copy)
    for copy in copies:
        copy.wait()
    pairs = heads * users
    cands = cquery.shape[0] // users
    for u in range(users):
        for h in range(heads):
            r = h * users + u
            rows = pl.ds(r * DH, DH)
            state = pieces[0, r * DH:(r + 1) * DH, :].astype(F32)
            prefix = jnp.zeros((DH, DH), F32)
            for p in range(1, ctx_count):
                prefix = jnp.where(me == p, state, prefix)
                base = pairs * DH + 3 * r
                log = pieces[p, pairs * DH:, :].astype(F32)
                log = jnp.sum(log[3 * r:3 * r + 3, :], axis=0, keepdims=True)
                state = jnp.exp(log) * state + pieces[p, r * DH:(r + 1) * DH, :].astype(F32)
            prefix_out[r * DH:(r + 1) * DH, :] = prefix.astype(BF16)
            lanes = slice(h * DH, (h + 1) * DH)
            crow = slice(u * cands, (u + 1) * cands)
            read = dot(cquery[crow, lanes], state.astype(BF16))
            value = scale_rms(read, gain_ref[lanes][None, :]) + own[crow, lanes].astype(F32)
            feat[crow, lanes] = value.astype(BF16)
    mine = lax.axis_index("head")
    share = cands // head_count
    for k in range(head_count):
        start = pl.multiple_of(dest(mine, k, head_count) * share, share)
        for u in range(users):
            feat_outs[k][u * share:(u + 1) * share, :] = feat[pl.ds(u * cands + start, share), :]


def kernel_d(users, heads, span, within, query, gate, prefix, cum_col, gain_ref, out):
    for u in range(users):
        for h in range(heads):
            r = h * users + u
            rows = slice(u * span, (u + 1) * span)
            lanes = slice(h * DH, (h + 1) * DH)
            carried = dot(query[rows, lanes], prefix[r * DH:(r + 1) * DH, :])
            readout = within[rows, lanes] + carried * jnp.exp(cum_col[:, r:r + 1])
            wide = gate[rows, lanes].astype(F32)
            value = scale_rms(readout, gain_ref[lanes][None, :]) * (wide * jax.nn.sigmoid(wide))
            out[u, :, lanes] = value.astype(BF16)


def kernel_e(users, head_count, *refs):
    feats = refs[:head_count]
    weights = refs[head_count:2 * head_count]
    second, out = refs[2 * head_count:2 * head_count + 2]
    hidden = dot(feats[0][...], weights[0][...])
    for k in range(1, head_count):
        hidden = hidden + dot(feats[k][...], weights[k][...])
    value = hidden * jax.nn.sigmoid(hidden) * second[...].astype(F32)[None, :]
    score = jnp.sum(value, axis=-1, keepdims=True)
    share = score.shape[0] // users
    row_id = lax.broadcasted_iota(jnp.int32, (share, share), 0)
    col_id = lax.broadcasted_iota(jnp.int32, (share, share), 1)
    for u in range(users):
        part = jnp.broadcast_to(score[u * share:(u + 1) * share, :], (share, share))
        out[u:u + 1, :] = jnp.sum(jnp.where(row_id == col_id, part, 0.0), axis=0, keepdims=True)


def is_power(n):
    return n & (n - 1) == 0


def source(index, k, n):
    return index ^ k if is_power(n) else lax.rem(index - k + n, n)


def dest(index, k, n):
    return index ^ k if is_power(n) else lax.rem(index + k, n)


def shift(array, axis, k, n):
    pairs = [(i, i ^ k if is_power(n) else (i + k) % n) for i in range(n)]
    return lax.ppermute(array, axis, pairs)


def local(
    behavior_embed,
    behavior_mask,
    history_len,
    log_decay,
    candidate_embed,
    input_weight,
    input_gain,
    proj_weight,
    output_gain,
    ranker_first,
    ranker_second,
):
    users, span = behavior_mask.shape
    cands = candidate_embed.shape[1]
    width = input_weight.shape[0]
    model = input_weight.shape[1]
    cols = proj_weight.shape[2]
    heads = cols // DH
    pairs = heads * users
    ctx_count = lax.axis_size("ctx")
    head_count = lax.axis_size("head")
    rows = users * span
    share = cands // head_count
    row_pad = -(-pairs // 8) * 8
    tail = -(-3 * pairs // 16) * 16
    payload_rows = pairs * DH + tail
    sds = jax.ShapeDtypeStruct

    norm, key, value, payload, cum, valid, cum_col = call(
        functools.partial(kernel_a, users, heads, span, span * ctx_count),
        (
            sds((rows, model), BF16),
            sds((rows, cols), BF16),
            sds((rows, cols), BF16),
            sds((payload_rows, DH), BF16),
            sds((row_pad, span), F32),
            sds((users, span), F32),
            sds((span, row_pad), F32),
        ),
        (history_len, behavior_mask, log_decay, behavior_embed, input_weight, input_gain,
         proj_weight),
        [SMEM, VMEM, VMEM, HBM, HBM, VMEM, HBM],
        (VMEM,) * 7,
        [
            pltpu.VMEM((users, span, width), BF16),
            pltpu.VMEM((width, model), BF16),
            pltpu.VMEM((2, model, cols), BF16),
            pltpu.VMEM((row_pad, span), F32),
            pltpu.SemaphoreType.DMA((3 + users,)),
        ],
        "features",
        2 * rows * model * (width + 2 * cols),
    )

    pieces = [payload] + [shift(payload, "ctx", k, ctx_count) for k in range(1, ctx_count)]
    forward = is_power(head_count)
    early, _ = lax.optimization_barrier((ranker_first, payload))
    weights = [ranker_first] + [None] * (head_count - 1)
    for k in range(1, head_count):
        if not (forward and k % 2 and k > 1):
            weights[k] = shift(early, "head", k, head_count)

    query, gate, within, cquery, own = call(
        functools.partial(kernel_b, users, heads, span),
        (
            sds((rows, cols), BF16),
            sds((rows, cols), BF16),
            sds((rows, cols), F32),
            sds((users * cands, cols), BF16),
            sds((users * cands, cols), BF16),
        ),
        (norm, key, value, cum, valid, cum_col, proj_weight, candidate_embed, input_weight,
         input_gain),
        [VMEM, VMEM, VMEM, VMEM, VMEM, VMEM, HBM, VMEM, VMEM, VMEM],
        (VMEM,) * 5,
        [
            pltpu.VMEM((model, cols), BF16),
            pltpu.VMEM((model, cols), BF16),
            pltpu.VMEM((users * cands, model), BF16),
            pltpu.SemaphoreType.DMA((2,)),
        ],
        "within",
        2 * rows * model * 2 * cols + 2 * rows * span * cols * 2,
    )

    prefix, *feats = call(
        functools.partial(kernel_c, users, heads, ctx_count, head_count, source, dest),
        (sds((pairs * DH, DH), BF16),) + (sds((users * share, cols), BF16),) * head_count,
        (*pieces, cquery, own, output_gain),
        [ANY] * ctx_count + [VMEM] * 3,
        (VMEM,) * (1 + head_count),
        [
            pltpu.VMEM((ctx_count, payload_rows, DH), BF16),
            pltpu.VMEM((users * cands, cols), BF16),
            pltpu.SemaphoreType.DMA((ctx_count,)),
        ],
        "final",
        2 * users * cands * cols * DH,
    )

    for k in range(1, head_count):
        if weights[k] is None:
            piece, _ = lax.optimization_barrier((weights[k - 1], prefix))
            weights[k] = shift(piece, "head", 1, head_count)
    feats = [feats[0]] + [shift(feats[k], "head", k, head_count) for k in range(1, head_count)]

    history_out = call(
        functools.partial(kernel_d, users, heads, span),
        sds((users, span, cols), BF16),
        (within, query, gate, prefix, cum_col, output_gain),
        [VMEM] * 6,
        VMEM,
        [],
        "carried",
        2 * rows * cols * DH,
    )

    scores = call(
        functools.partial(kernel_e, users, head_count),
        sds((users, share), F32),
        (*feats, *weights, ranker_second),
        [VMEM] * (2 * head_count + 1),
        VMEM,
        [],
        "scores",
        2 * users * share * model * ranker_first.shape[1],
    )
    return (history_out, scores)


def solution(mesh):
    in_specs = (
        P("grp", "ctx", None),
        P("grp", "ctx"),
        P("grp"),
        P("head", "grp", "ctx"),
        P("grp", "ctx", None),
        P(),
        P(),
        P(None, None, "head"),
        P("head"),
        P("head", None),
        P(),
    )
    out_specs = (P("grp", "ctx", "head"), P("grp", ("ctx", "head")))
    return jax.shard_map(local, mesh=mesh, in_specs=in_specs, out_specs=out_specs, check_vma=False)
```
